32 devices in a mesh: node: 4 (over z), dom: 8 (over y, x, core).
Axes of the slice: x: 2, y: 2, z: 4, core: 2. Of those that a mesh axis runs over, the one named last changes fastest.
Arguments:
- probes: float32 [32, 16, 16, 128], P(None, 'dom'), may hold values from -24 to 24
- slope: float32 [16, 16, 128], P('dom'), may hold values from 4 to 6
- root: float32 [16, 16, 128], P('dom'), may hold values from 0.3 to 0.7
- damping: float32 [16, 16, 128], P('dom'), may hold values from 0.3 to 1.2
Outputs:
- moments: float32 [2, 2, 32, 16, 16, 128], P(None, None, 'node', 'dom')
- projections: float32 [2, 2, 32, 32], replicated
The draws below stay inside these ranges and needn't reach their ends.
All inputs are finite; a program needn't handle non-finite values.
Results may differ from the reference program's by a relative error of at most 0.00013.
Values sent between devices are 32-bit elements; how exact they have to be, the bound alone decides.
A program may use at most 64 MiB of HBM per device.

```python
import math
import jax
import jax.numpy as jnp
from jax import lax

P_SIZE = 32
NY = 16
NZ = 128
SWEEPS = 8
NODES = 8
NX = 16


def block_scale(stream_key, shape, cuts, least, largest):
    gain, own = 1.0, jax.random.fold_in(stream_key, 6)
    for position, shards_of in cuts:
        heights = jnp.exp(jax.random.uniform(jax.random.fold_in(own, position), (shards_of,), jnp.float32, least / len(cuts), largest / len(cuts)))
        gain = gain * jnp.repeat(heights, shape[position] // shards_of).reshape([-1 if axis == position else 1 for axis in range(len(shape))])
    return gain


def gaussian(own_key, shape, deviation, reach, shards=(), dtype=jnp.bfloat16):
    factor_of = block_scale(own_key, shape, shards, -0.22, 0.18) if shards else 1.0
    values = jax.random.normal(own_key, shape, jnp.float32) * deviation * factor_of
    return jnp.minimum(jnp.maximum(values, -reach), reach).astype(dtype)


def setup_inputs(seed: int = 0) -> dict:
    seeds = jax.random.split(jax.random.key(seed), 5)
    probes = gaussian(seeds[0], (P_SIZE, NX, NY, NZ), 4.0, 24.0, ((1, 8),), jnp.float32)
    slope = jnp.clip(jnp.exp(math.log(6.0) - 0.4054651 * jax.random.uniform(seeds[1], (NX, NY, NZ), jnp.float32) ** block_scale(seeds[1], (NX, NY, NZ), ((0, 8),), -0.2, 0.2)), 4.0, 6.0)
    root = jnp.clip(0.3 + 0.39999998 * jax.random.uniform(seeds[2], (NX, NY, NZ), jnp.float32) ** block_scale(seeds[2], (NX, NY, NZ), ((0, 8),), -0.2, 0.2), 0.3, 0.7)
    damping = jnp.clip(jnp.exp(math.log(1.2) - 1.3862944 * jax.random.uniform(seeds[3], (NX, NY, NZ), jnp.float32) ** block_scale(seeds[3], (NX, NY, NZ), ((0, 8),), -0.2, 0.2)), 0.3, 1.2)
    return dict(probes=probes, slope=slope, root=root, damping=damping)


CENTRE = 0.5
RADIUS = 2.0


def neighbour_sum(field):
    padded = jnp.pad(field, ((0, 0), (1, 1), (1, 1), (1, 1)))
    total = padded[:, 2:, 1:-1, 1:-1] + padded[:, :-2, 1:-1, 1:-1]
    total = total + padded[:, 1:-1, 2:, 1:-1] + padded[:, 1:-1, :-2, 1:-1]
    return total + padded[:, 1:-1, 1:-1, 2:] + padded[:, 1:-1, 1:-1, :-2]


def reference(probes, slope, root, damping):
    vectors = probes.shape[0]
    moments = jnp.zeros((2, 2) + probes.shape, jnp.float32)
    for node in range(NODES):
        theta = 2.0 * math.pi * (node + 0.5) / NODES
        shift_real = CENTRE + RADIUS * math.cos(theta)
        shift_imaginary = RADIUS * math.sin(theta)
        decay = math.exp(-shift_real)
        real_d = slope * (shift_real - root) + damping * (decay * math.cos(shift_imaginary))
        imag_d = slope * shift_imaginary - damping * (decay * math.sin(shift_imaginary))
        scale = 1.0 / (real_d * real_d + imag_d * imag_d)
        qre = real_d * scale
        qim = -imag_d * scale
        iterate_real = probes * qre
        iterate_imaginary = probes * qim
        for sweep in range(SWEEPS):
            bre = probes + neighbour_sum(iterate_real)
            bim = neighbour_sum(iterate_imaginary)
            iterate_real, iterate_imaginary = bre * qre - bim * qim, bre * qim + bim * qre
        residual_real = RADIUS * math.cos(theta) / NODES
        residual_imaginary = RADIUS * math.sin(theta) / NODES
        update_real = residual_real * shift_real - residual_imaginary * shift_imaginary
        update_imaginary = residual_real * shift_imaginary + residual_imaginary * shift_real
        first = jnp.stack([residual_real * iterate_real - residual_imaginary * iterate_imaginary, residual_real * iterate_imaginary + residual_imaginary * iterate_real])
        second_moment = jnp.stack([update_real * iterate_real - update_imaginary * iterate_imaginary, update_real * iterate_imaginary + update_imaginary * iterate_real])
        moments = moments + jnp.stack([first, second_moment])
    flat = moments.reshape(4 * vectors, -1)
    basis = probes.reshape(vectors, -1)
    partial_value = lax.dot_general(flat, basis, (((1,), (1,)), ((), ())), precision=lax.Precision.HIGHEST, preferred_element_type=jnp.float32)
    projections = partial_value.reshape(2, 2, vectors, vectors) / (NX * NY * NZ)
    return moments, projections
```

```python
import functools
import math

import jax
import jax.numpy as jnp
from jax import lax
from jax.experimental import pallas as pl
from jax.experimental.pallas import tpu as pltpu
from jax.sharding import PartitionSpec as P

NODE_DEV = 2
SWEEPS = 8
UNROLL = 2


CENTRE = 0.5
RADIUS = 2.0


def grid_step(source, fields, factor_re, factor_im):
    padded = jnp.pad(fields, ((0, 0), (0, 0), (1, 1), (1, 1), (1, 1)))
    total = padded[:, :, 2:, 1:-1, 1:-1] + padded[:, :, :-2, 1:-1, 1:-1]
    total = total + padded[:, :, 1:-1, 2:, 1:-1] + padded[:, :, 1:-1, :-2, 1:-1]
    total = total + padded[:, :, 1:-1, 1:-1, 2:] + padded[:, :, 1:-1, 1:-1, :-2]
    real_part = source + total[:, 0]
    imag_part = total[:, 1]
    return jnp.stack(
        [
            real_part * factor_re - imag_part * factor_im,
            real_part * factor_im + imag_part * factor_re,
        ],
        axis=1,
    )


def inverse_diagonal(shift_real, shift_imaginary, slope, root, damping, guard):
    zr_col = shift_real[:, None, None, None, None]
    zi_col = shift_imaginary[:, None, None, None, None]
    decay = jnp.exp(-zr_col)
    real_d = slope * (zr_col - root) + damping * (decay * jnp.cos(zi_col))
    imag_d = slope * zi_col - damping * (decay * jnp.sin(zi_col))
    scale = 1.0 / (real_d * real_d + imag_d * imag_d + guard)
    return (real_d * scale, -imag_d * scale)


def per_system(fields, weight_re, weight_im):
    a_col = weight_re[:, None, None, None]
    b_col = weight_im[:, None, None, None]
    return jnp.stack(
        [a_col * fields[:, 0] - b_col * fields[:, 1], a_col * fields[:, 1] + b_col * fields[:, 0]]
    )


def body(probes, slope, root, damping):
    vectors = probes.shape[0]
    planes = probes.shape[1]
    groups = lax.axis_size("node")
    total = NODE_DEV * groups
    first = (lax.axis_index("node") * NODE_DEV).astype(jnp.float32)
    dom_size = lax.axis_size("dom")
    count = NODE_DEV * vectors // dom_size
    replicated = jnp.broadcast_to(probes[None], (NODE_DEV,) + probes.shape).reshape(
        (NODE_DEV * vectors,) + probes.shape[1:]
    )
    own = lax.all_to_all(replicated, "dom", split_axis=0, concat_axis=1, tiled=True)
    slope_all, root_all, damping_all = (
        lax.all_gather(slope, "dom", axis=0, tiled=True),
        lax.all_gather(root, "dom", axis=0, tiled=True),
        lax.all_gather(damping, "dom", axis=0, tiled=True),
    )
    system = lax.axis_index("dom") * count + jnp.arange(count)
    position = first + (system // vectors).astype(jnp.float32)
    theta = 2.0 * math.pi * (position + 0.5) / total
    shift_real = CENTRE + RADIUS * jnp.cos(theta)
    shift_imaginary = RADIUS * jnp.sin(theta)
    qre, qim = inverse_diagonal(
        shift_real, shift_imaginary, slope_all[None], root_all[None], damping_all[None], 0.0
    )
    qre = qre[:, 0]
    qim = qim[:, 0]
    fields = jnp.stack([own * qre, own * qim], axis=1)
    for sweep in range(SWEEPS):
        fields = grid_step(own, fields, qre, qim)
    weight_re = RADIUS * jnp.cos(theta) / total
    weight_im = RADIUS * jnp.sin(theta) / total
    shifted_re = weight_re * shift_real - weight_im * shift_imaginary
    shifted_im = weight_re * shift_imaginary + weight_im * shift_real
    terms = jnp.stack(
        [per_system(fields, weight_re, weight_im), per_system(fields, shifted_re, shifted_im)]
    )
    back = lax.all_to_all(terms, "dom", split_axis=3, concat_axis=2, tiled=True)
    local = jnp.sum(back.reshape((2, 2, NODE_DEV, vectors) + probes.shape[1:]), axis=2)
    flat = local.reshape(4 * vectors, -1)
    basis = probes.reshape(vectors, -1)
    partial_value = lax.dot_general(
        flat,
        basis,
        (((1,), (1,)), ((), ())),
        precision=lax.Precision.HIGHEST,
        preferred_element_type=jnp.float32,
    )
    cells = planes * probes.shape[2] * probes.shape[3] * lax.axis_size("dom")
    projections = lax.psum(partial_value.reshape(2, 2, vectors, vectors) / cells, ("node", "dom"))
    summed = lax.psum(local, "node")
    share = vectors // groups
    moments = lax.dynamic_slice_in_dim(summed, lax.axis_index("node") * share, share, 2)
    return (moments, projections)


MESH = pl.DeviceIdType.MESH


def contour(total):
    nodes = []
    for node in range(total // 2):
        theta = 2.0 * math.pi * (node + 0.5) / total
        zr, zi = CENTRE + RADIUS * math.cos(theta), RADIUS * math.sin(theta)
        wr, wi = RADIUS * math.cos(theta) / total, RADIUS * math.sin(theta) / total
        decay = math.exp(-zr)
        nodes.append(
            dict(
                zr=zr,
                zi=zi,
                er=decay * math.cos(zi),
                ei=decay * math.sin(zi),
                first=(2.0 * wr, 2.0 * wi),
                second=(2.0 * (wr * zr - wi * zi), 2.0 * (wr * zi + wi * zr)),
            )
        )
    return nodes


def kernel(
    nodes,
    groups,
    doms,
    planes,
    ny,
    probes_ref,
    slope_ref,
    root_ref,
    damping_ref,
    moments_ref,
    projections_ref,
    coef,
    rhs,
    local,
    basis,
    q,
    even,
    odd,
    outgoing,
    incoming,
    partial,
    gathered,
    shared,
    own_sem,
    field_send,
    field_recv,
    term_send,
    term_recv,
    dom_send,
    dom_recv,
    node_send,
    node_recv,
    out_sem,
):
    g = lax.axis_index("node")
    d = lax.axis_index("dom")
    rows = planes * ny
    half = len(nodes)
    nx = doms * planes
    nz = rhs.shape[-1]
    fields = (slope_ref, root_ref, damping_ref)

    barrier = pltpu.get_barrier_semaphore()
    for r in range(1, doms):
        pl.semaphore_signal(barrier, inc=1, device_id={"dom": d ^ r}, device_id_type=MESH)
    for s in range(1, groups):
        pl.semaphore_signal(
            barrier, inc=1, device_id={"node": lax.rem(g + s, groups)}, device_id_type=MESH
        )

    mine = pl.ds(pl.multiple_of(d * rows, rows), rows)
    own = [pltpu.make_async_copy(f, coef.at[i, mine], own_sem.at[i]) for i, f in enumerate(fields)]
    own.append(
        pltpu.make_async_copy(
            probes_ref.at[pl.ds((g * doms + d) * rows, rows)], rhs.at[mine], own_sem.at[3]
        )
    )
    whole_local = pltpu.make_async_copy(probes_ref, local, own_sem.at[4])
    for copy in own:
        copy.start()
    whole_local.start()
    pl.semaphore_wait(barrier, doms - 1 + groups - 1)

    sends = {}
    for r in range(doms - 1, 0, -1):
        e = d ^ r
        pieces = []
        for i, f in enumerate(fields):
            pieces.append((f, coef.at[i, mine]))
        pieces.append((probes_ref.at[pl.ds((g * doms + e) * rows, rows)], rhs.at[mine]))
        for i, (src, dst) in enumerate(pieces):
            copy = pltpu.make_async_remote_copy(
                src_ref=src,
                dst_ref=dst,
                send_sem=field_send.at[r, i],
                recv_sem=field_recv.at[r, i],
                device_id={"dom": e},
                device_id_type=MESH,
            )
            copy.start()
            sends[r, i] = copy

    blank = jnp.zeros((2, 8, nz), jnp.float32)
    for buffer in (even, odd):
        for k in range(half):
            for end in (0, nx + 1):
                buffer[k, :, end] = jnp.zeros((2, ny + 16, nz), jnp.float32)

            def clear(x, _, buffer=buffer, k=k):
                buffer[k, :, x, 0:8] = blank
                buffer[k, :, x, ny + 8 : ny + 16] = blank
                return 0

            lax.fori_loop(1, nx + 1, clear, 0)
    partial[...] = jnp.zeros(partial.shape, jnp.float32)

    lane = lax.broadcasted_iota(jnp.int32, (ny, nz), 1)
    first_lane, last_lane = lane == 0, lane == nz - 1

    def start_plane(x):
        at = pl.ds(pl.multiple_of(x * ny, ny), ny)
        slope, root, damping = coef[0, at], coef[1, at], coef[2, at]
        b = rhs[at]
        for k, c in enumerate(nodes):
            re = slope * (c["zr"] - root) + damping * c["er"]
            im = slope * c["zi"] - damping * c["ei"]
            scale = 1.0 / (re * re + im * im)
            re = re * scale
            im = -im * scale
            q[k, 0, at] = re
            q[k, 1, at] = im
            even[k, 0, x + 1, 8 : ny + 8] = b * re
            even[k, 1, x + 1, 8 : ny + 8] = b * im

    for copy in own:
        copy.wait()
    for p in range(planes):
        start_plane(d * planes + p)

    whole_local.wait()
    vectors = local.shape[0] // rows
    for t in range(rows):
        values = local[pl.ds(t, vectors, stride=rows), :]
        high = values.astype(jnp.bfloat16)
        low = (values - high.astype(jnp.float32)).astype(jnp.bfloat16)
        basis[0, :, t * nz : (t + 1) * nz] = high
        basis[1, :, t * nz : (t + 1) * nz] = low

    for r in range(1, doms):
        for i in range(4):
            sends[r, i].wait_recv()
        for p in range(planes):
            start_plane((d ^ r) * planes + p)

    def neighbours(source, k, c, x):
        centre = source[k, c, x + 1, 8 : ny + 8]
        total = source[k, c, x, 8 : ny + 8] + source[k, c, x + 2, 8 : ny + 8]
        total = total + (source[k, c, x + 1, 7 : ny + 7] + source[k, c, x + 1, 9 : ny + 9])
        before = jnp.where(first_lane, 0.0, pltpu.roll(centre, 1, 1))
        after = jnp.where(last_lane, 0.0, pltpu.roll(centre, nz - 1, 1))
        return total + (before + after)

    def update(source, k, x, b):
        at = pl.ds(pl.multiple_of(x * ny, ny), ny)
        re = b + neighbours(source, k, 0, x)
        im = neighbours(source, k, 1, x)
        qre, qim = q[k, 0, at], q[k, 1, at]
        return re * qre - im * qim, re * qim + im * qre

    def sweep(source, target):
        def step(i, _):
            for u in range(UNROLL):
                x = i * UNROLL + u
                b = rhs[pl.ds(pl.multiple_of(x * ny, ny), ny)]
                for k in range(half):
                    re, im = update(source, k, x, b)
                    target[k, 0, x + 1, 8 : ny + 8] = re
                    target[k, 1, x + 1, 8 : ny + 8] = im
            return 0

        lax.fori_loop(0, nx // UNROLL, step, 0)

    def pair(_, carry):
        sweep(even, odd)
        sweep(odd, even)
        return carry

    lax.fori_loop(0, (SWEEPS - 1) // 2, pair, 0)
    source = even
    if (SWEEPS - 1) % 2:
        sweep(even, odd)
        source = odd

    backs = {}

    def send_terms(r):
        copy = pltpu.make_async_remote_copy(
            src_ref=outgoing.at[r],
            dst_ref=incoming.at[:, mine],
            send_sem=term_send.at[r],
            recv_sem=term_recv.at[r],
            device_id={"dom": d ^ r},
            device_id_type=MESH,
        )
        copy.start()
        backs[r] = copy

    for r in range(doms - 1, -1, -1):
        for p in range(planes):
            x = (d ^ r) * planes + p
            b = rhs[pl.ds(pl.multiple_of(x * ny, ny), ny)]
            first = second = None
            for k, c in enumerate(nodes):
                re, im = update(source, k, x, b)
                one = re * c["first"][0] - im * c["first"][1]
                two = re * c["second"][0] - im * c["second"][1]
                first = one if first is None else first + one
                second = two if second is None else second + two
            if r:
                outgoing[r, 0, p * ny : (p + 1) * ny] = first
                outgoing[r, 1, p * ny : (p + 1) * ny] = second
            else:
                at = pl.ds(pl.multiple_of(d * rows + p * ny, ny), ny)
                incoming[0, at] = first
                incoming[1, at] = second
        if r + 1 < doms:
            send_terms(r + 1)

    for r in range(doms - 1, 0, -1):
        backs[r].wait_recv()
    result = pltpu.make_async_copy(incoming, moments_ref, out_sem)
    result.start()

    highs, lows = [], []
    for t in range(rows):
        values = jnp.concatenate(
            [incoming[m, pl.ds(t, doms, stride=rows), :] for m in range(2)], axis=0
        )
        high = values.astype(jnp.bfloat16)
        highs.append(high)
        lows.append((values - high.astype(jnp.float32)).astype(jnp.bfloat16))
    left = jnp.concatenate([jnp.concatenate(highs, axis=1), jnp.concatenate(lows, axis=1)], axis=0)
    dims = (((1,), (1,)), ((), ()))
    product = lax.dot_general(
        left, basis[0], dims, preferred_element_type=jnp.float32
    ) + lax.dot_general(left, basis[1], dims, preferred_element_type=jnp.float32)
    product = (product[: 2 * doms] + product[2 * doms :]) * (1.0 / (nx * ny * nz))
    partial[:, :vectors] = product
    gathered[d] = partial[...]

    copies = []
    for r in range(doms - 1, 0, -1):
        copy = pltpu.make_async_remote_copy(
            src_ref=partial,
            dst_ref=gathered.at[d],
            send_sem=dom_send.at[r],
            recv_sem=dom_recv.at[r],
            device_id={"dom": d ^ r},
            device_id_type=MESH,
        )
        copy.start()
        copies.append(copy)
    for copy in copies:
        copy.wait_recv()
    total = gathered[0]
    for e in range(1, doms):
        total = total + gathered[e]
    shared[g] = total
    spread = []
    for s in range(1, groups):
        copy = pltpu.make_async_remote_copy(
            src_ref=shared.at[g],
            dst_ref=shared.at[g],
            send_sem=node_send.at[s],
            recv_sem=node_recv.at[s],
            device_id={"node": lax.rem(g + s, groups)},
            device_id_type=MESH,
        )
        copy.start()
        spread.append(copy)
    for r in range(1, doms):
        for i in range(4):
            sends[r, i].wait_send()
        backs[r].wait_send()
    for copy in copies:
        copy.wait_send()
    for copy in spread:
        copy.wait()
    for n in range(groups):
        for m in range(2):
            projections_ref[m, n * doms : (n + 1) * doms, :] = shared[n, m * doms : (m + 1) * doms, :vectors]
    result.wait()


def fused(total, groups, doms, probes, slope, root, damping):
    vectors, planes, ny, nz = probes.shape
    rows, nx, half = planes * ny, planes * doms, total // 2
    anywhere = pl.BlockSpec(memory_space=pl.ANY)
    grid = (half, 2, nx + 2, ny + 16, nz)
    moments, projections = pl.pallas_call(
        functools.partial(kernel, contour(total), groups, doms, planes, ny),
        out_shape=(
            jax.ShapeDtypeStruct((2, doms * rows, nz), jnp.float32),
            jax.ShapeDtypeStruct((2, vectors, vectors), jnp.float32),
        ),
        in_specs=[anywhere] * 4,
        out_specs=(anywhere, pl.BlockSpec(memory_space=pltpu.VMEM)),
        scratch_shapes=[
            pltpu.VMEM((3, nx * ny, nz), jnp.float32),
            pltpu.VMEM((nx * ny, nz), jnp.float32),
            pltpu.VMEM((vectors * rows, nz), jnp.float32),
            pltpu.VMEM((2, vectors, rows * nz), jnp.bfloat16),
            pltpu.VMEM((half, 2, nx * ny, nz), jnp.float32),
            pltpu.VMEM(grid, jnp.float32),
            pltpu.VMEM(grid, jnp.float32),
            pltpu.VMEM((doms, 2, rows, nz), jnp.float32),
            pltpu.VMEM((2, doms * rows, nz), jnp.float32),
            pltpu.VMEM((2 * doms, 128), jnp.float32),
            pltpu.VMEM((doms, 2 * doms, 128), jnp.float32),
            pltpu.VMEM((groups, 2 * doms, 128), jnp.float32),
            pltpu.SemaphoreType.DMA((5,)),
            pltpu.SemaphoreType.DMA((doms, 4)),
            pltpu.SemaphoreType.DMA((doms, 4)),
            pltpu.SemaphoreType.DMA((doms,)),
            pltpu.SemaphoreType.DMA((doms,)),
            pltpu.SemaphoreType.DMA((doms,)),
            pltpu.SemaphoreType.DMA((doms,)),
            pltpu.SemaphoreType.DMA((groups,)),
            pltpu.SemaphoreType.DMA((groups,)),
            pltpu.SemaphoreType.DMA,
        ],
        compiler_params=pltpu.CompilerParams(collective_id=0, has_side_effects=True),
    )(
        probes.reshape(vectors * rows, nz),
        slope.reshape(rows, nz),
        root.reshape(rows, nz),
        damping.reshape(rows, nz),
    )
    moments = moments.reshape(2, 1, doms, planes, ny, nz)
    moments = jnp.pad(moments, ((0, 0), (0, 1)) + ((0, 0),) * 4)
    projections = jnp.pad(projections[:, None], ((0, 0), (0, 1), (0, 0), (0, 0)))
    return moments, projections


def solution(mesh):
    groups, doms = mesh.shape["node"], mesh.shape["dom"]

    def step(probes, slope, root, damping):
        vectors, ny = probes.shape[0], probes.shape[2]
        one_each = vectors == groups * doms and doms & (doms - 1) == 0 and doms % 8 == 0
        if one_each and ny % 8 == 0 and vectors <= 128 and probes.shape[3] % 128 == 0:
            return fused(NODE_DEV * groups, groups, doms, probes, slope, root, damping)
        return body(probes, slope, root, damping)

    in_specs = (
        P(None, "dom", None, None),
        P("dom", None, None),
        P("dom", None, None),
        P("dom", None, None),
    )
    out_specs = (P(None, None, "node", "dom", None, None), P())
    return jax.shard_map(step, mesh=mesh, in_specs=in_specs, out_specs=out_specs, check_vma=False)
```

```python
import functools
import math

import jax
import jax.numpy as jnp
from jax import lax
from jax.experimental import pallas as pl
from jax.experimental.pallas import tpu as pltpu
from jax.sharding import PartitionSpec as P

NODE_DEV = 2
SWEEPS = 8
UNROLL = 16


CENTRE = 0.5
RADIUS = 2.0


def grid_step(source, fields, factor_re, factor_im):
    padded = jnp.pad(fields, ((0, 0), (0, 0), (1, 1), (1, 1), (1, 1)))
    total = padded[:, :, 2:, 1:-1, 1:-1] + padded[:, :, :-2, 1:-1, 1:-1]
    total = total + padded[:, :, 1:-1, 2:, 1:-1] + padded[:, :, 1:-1, :-2, 1:-1]
    total = total + padded[:, :, 1:-1, 1:-1, 2:] + padded[:, :, 1:-1, 1:-1, :-2]
    real_part = source + total[:, 0]
    imag_part = total[:, 1]
    return jnp.stack(
        [
            real_part * factor_re - imag_part * factor_im,
            real_part * factor_im + imag_part * factor_re,
        ],
        axis=1,
    )


def inverse_diagonal(shift_real, shift_imaginary, slope, root, damping, guard):
    zr_col = shift_real[:, None, None, None, None]
    zi_col = shift_imaginary[:, None, None, None, None]
    decay = jnp.exp(-zr_col)
    real_d = slope * (zr_col - root) + damping * (decay * jnp.cos(zi_col))
    imag_d = slope * zi_col - damping * (decay * jnp.sin(zi_col))
    scale = 1.0 / (real_d * real_d + imag_d * imag_d + guard)
    return (real_d * scale, -imag_d * scale)


def per_system(fields, weight_re, weight_im):
    a_col = weight_re[:, None, None, None]
    b_col = weight_im[:, None, None, None]
    return jnp.stack(
        [a_col * fields[:, 0] - b_col * fields[:, 1], a_col * fields[:, 1] + b_col * fields[:, 0]]
    )


def body(probes, slope, root, damping):
    vectors = probes.shape[0]
    planes = probes.shape[1]
    groups = lax.axis_size("node")
    total = NODE_DEV * groups
    first = (lax.axis_index("node") * NODE_DEV).astype(jnp.float32)
    dom_size = lax.axis_size("dom")
    count = NODE_DEV * vectors // dom_size
    replicated = jnp.broadcast_to(probes[None], (NODE_DEV,) + probes.shape).reshape(
        (NODE_DEV * vectors,) + probes.shape[1:]
    )
    own = lax.all_to_all(replicated, "dom", split_axis=0, concat_axis=1, tiled=True)
    slope_all, root_all, damping_all = (
        lax.all_gather(slope, "dom", axis=0, tiled=True),
        lax.all_gather(root, "dom", axis=0, tiled=True),
        lax.all_gather(damping, "dom", axis=0, tiled=True),
    )
    system = lax.axis_index("dom") * count + jnp.arange(count)
    position = first + (system // vectors).astype(jnp.float32)
    theta = 2.0 * math.pi * (position + 0.5) / total
    shift_real = CENTRE + RADIUS * jnp.cos(theta)
    shift_imaginary = RADIUS * jnp.sin(theta)
    qre, qim = inverse_diagonal(
        shift_real, shift_imaginary, slope_all[None], root_all[None], damping_all[None], 0.0
    )
    qre = qre[:, 0]
    qim = qim[:, 0]
    fields = jnp.stack([own * qre, own * qim], axis=1)
    for sweep in range(SWEEPS):
        fields = grid_step(own, fields, qre, qim)
    weight_re = RADIUS * jnp.cos(theta) / total
    weight_im = RADIUS * jnp.sin(theta) / total
    shifted_re = weight_re * shift_real - weight_im * shift_imaginary
    shifted_im = weight_re * shift_imaginary + weight_im * shift_real
    terms = jnp.stack(
        [per_system(fields, weight_re, weight_im), per_system(fields, shifted_re, shifted_im)]
    )
    back = lax.all_to_all(terms, "dom", split_axis=3, concat_axis=2, tiled=True)
    local = jnp.sum(back.reshape((2, 2, NODE_DEV, vectors) + probes.shape[1:]), axis=2)
    flat = local.reshape(4 * vectors, -1)
    basis = probes.reshape(vectors, -1)
    partial_value = lax.dot_general(
        flat,
        basis,
        (((1,), (1,)), ((), ())),
        precision=lax.Precision.HIGHEST,
        preferred_element_type=jnp.float32,
    )
    cells = planes * probes.shape[2] * probes.shape[3] * lax.axis_size("dom")
    projections = lax.psum(partial_value.reshape(2, 2, vectors, vectors) / cells, ("node", "dom"))
    summed = lax.psum(local, "node")
    share = vectors // groups
    moments = lax.dynamic_slice_in_dim(summed, lax.axis_index("node") * share, share, 2)
    return (moments, projections)


MESH = pl.DeviceIdType.MESH


def contour(total):
    nodes = []
    for node in range(total // 2):
        theta = 2.0 * math.pi * (node + 0.5) / total
        zr, zi = CENTRE + RADIUS * math.cos(theta), RADIUS * math.sin(theta)
        wr, wi = RADIUS * math.cos(theta) / total, RADIUS * math.sin(theta) / total
        decay = math.exp(-zr)
        nodes.append(
            dict(
                zr=zr,
                zi=zi,
                er=decay * math.cos(zi),
                ei=decay * math.sin(zi),
                first=(2.0 * wr, 2.0 * wi),
                second=(2.0 * (wr * zr - wi * zi), 2.0 * (wr * zi + wi * zr)),
            )
        )
    return nodes


def kernel(
    nodes,
    groups,
    doms,
    planes,
    ny,
    probes_ref,
    slope_ref,
    root_ref,
    damping_ref,
    moments_ref,
    projections_ref,
    coef,
    rhs,
    local,
    basis,
    q,
    even,
    odd,
    outgoing,
    incoming,
    partial,
    gathered,
    shared,
    own_sem,
    field_send,
    field_recv,
    term_send,
    term_recv,
    dom_send,
    dom_recv,
    node_send,
    node_recv,
    out_sem,
):
    g = lax.axis_index("node")
    d = lax.axis_index("dom")
    rows = planes * ny
    half = len(nodes)
    nx = doms * planes
    nz = rhs.shape[-1]
    fields = (slope_ref, root_ref, damping_ref)

    barrier = pltpu.get_barrier_semaphore()
    for r in range(1, doms):
        pl.semaphore_signal(barrier, inc=1, device_id={"dom": d ^ r}, device_id_type=MESH)
    for s in range(1, groups):
        pl.semaphore_signal(
            barrier, inc=1, device_id={"node": lax.rem(g + s, groups)}, device_id_type=MESH
        )

    mine = pl.ds(pl.multiple_of(d * rows, rows), rows)
    own = [pltpu.make_async_copy(f, coef.at[i, mine], own_sem.at[i]) for i, f in enumerate(fields)]
    own.append(
        pltpu.make_async_copy(
            probes_ref.at[pl.ds((g * doms + d) * rows, rows)], rhs.at[mine], own_sem.at[3]
        )
    )
    whole_local = pltpu.make_async_copy(probes_ref, local, own_sem.at[4])
    for copy in own:
        copy.start()
    whole_local.start()
    pl.semaphore_wait(barrier, doms - 1 + groups - 1)

    sends = {}
    for r in range(doms - 1, 0, -1):
        e = d ^ r
        pieces = []
        for i, f in enumerate(fields):
            pieces.append((f, coef.at[i, mine]))
        pieces.append((probes_ref.at[pl.ds((g * doms + e) * rows, rows)], rhs.at[mine]))
        for i, (src, dst) in enumerate(pieces):
            copy = pltpu.make_async_remote_copy(
                src_ref=src,
                dst_ref=dst,
                send_sem=field_send.at[r, i],
                recv_sem=field_recv.at[r, i],
                device_id={"dom": e},
                device_id_type=MESH,
            )
            copy.start()
            sends[r, i] = copy

    blank = jnp.zeros((2, 8, nz), jnp.float32)
    for buffer in (even, odd):
        for k in range(half):
            for end in (0, nx + 1):
                buffer[k, :, end] = jnp.zeros((2, ny + 16, nz), jnp.float32)

            def clear(x, _, buffer=buffer, k=k):
                buffer[k, :, x, 0:8] = blank
                buffer[k, :, x, ny + 8 : ny + 16] = blank
                return 0

            lax.fori_loop(1, nx + 1, clear, 0)
    partial[...] = jnp.zeros(partial.shape, jnp.float32)

    lane = lax.broadcasted_iota(jnp.int32, (ny, nz), 1)
    first_lane, last_lane = lane == 0, lane == nz - 1

    def start_plane(x):
        at = pl.ds(pl.multiple_of(x * ny, ny), ny)
        slope, root, damping = coef[0, at], coef[1, at], coef[2, at]
        b = rhs[at]
        for k, c in enumerate(nodes):
            re = slope * (c["zr"] - root) + damping * c["er"]
            im = slope * c["zi"] - damping * c["ei"]
            scale = 1.0 / (re * re + im * im)
            re = re * scale
            im = -im * scale
            q[k, 0, at] = re
            q[k, 1, at] = im
            even[k, 0, x + 1, 8 : ny + 8] = b * re
            even[k, 1, x + 1, 8 : ny + 8] = b * im

    for copy in own:
        copy.wait()
    for p in range(planes):
        start_plane(d * planes + p)

    whole_local.wait()
    vectors = local.shape[0] // rows
    for t in range(rows):
        values = local[pl.ds(t, vectors, stride=rows), :]
        high = values.astype(jnp.bfloat16)
        low = (values - high.astype(jnp.float32)).astype(jnp.bfloat16)
        basis[0, :, t * nz : (t + 1) * nz] = high
        basis[1, :, t * nz : (t + 1) * nz] = low

    for r in range(1, doms):
        for i in range(4):
            sends[r, i].wait_recv()
        for p in range(planes):
            start_plane((d ^ r) * planes + p)

    def neighbours(source, k, c, x):
        centre = source[k, c, x + 1, 8 : ny + 8]
        total = source[k, c, x, 8 : ny + 8] + source[k, c, x + 2, 8 : ny + 8]
        total = total + (source[k, c, x + 1, 7 : ny + 7] + source[k, c, x + 1, 9 : ny + 9])
        before = jnp.where(first_lane, 0.0, pltpu.roll(centre, 1, 1))
        after = jnp.where(last_lane, 0.0, pltpu.roll(centre, nz - 1, 1))
        return total + (before + after)

    def update(source, k, x, b):
        at = pl.ds(pl.multiple_of(x * ny, ny), ny)
        re = b + neighbours(source, k, 0, x)
        im = neighbours(source, k, 1, x)
        qre, qim = q[k, 0, at], q[k, 1, at]
        return re * qre - im * qim, re * qim + im * qre

    def sweep(source, target):
        def step(i, _):
            for u in range(UNROLL):
                x = i * UNROLL + u
                b = rhs[pl.ds(pl.multiple_of(x * ny, ny), ny)]
                for k in range(half):
                    re, im = update(source, k, x, b)
                    target[k, 0, x + 1, 8 : ny + 8] = re
                    target[k, 1, x + 1, 8 : ny + 8] = im
            return 0

        lax.fori_loop(0, nx // UNROLL, step, 0)

    def pair(_, carry):
        sweep(even, odd)
        sweep(odd, even)
        return carry

    lax.fori_loop(0, (SWEEPS - 1) // 2, pair, 0)
    source = even
    if (SWEEPS - 1) % 2:
        sweep(even, odd)
        source = odd

    backs = {}

    def send_terms(r):
        copy = pltpu.make_async_remote_copy(
            src_ref=outgoing.at[r],
            dst_ref=incoming.at[:, mine],
            send_sem=term_send.at[r],
            recv_sem=term_recv.at[r],
            device_id={"dom": d ^ r},
            device_id_type=MESH,
        )
        copy.start()
        backs[r] = copy

    for r in range(doms - 1, -1, -1):
        for p in range(planes):
            x = (d ^ r) * planes + p
            b = rhs[pl.ds(pl.multiple_of(x * ny, ny), ny)]
            first = second = None
            for k, c in enumerate(nodes):
                re, im = update(source, k, x, b)
                one = re * c["first"][0] - im * c["first"][1]
                two = re * c["second"][0] - im * c["second"][1]
                first = one if first is None else first + one
                second = two if second is None else second + two
            if r:
                outgoing[r, 0, p * ny : (p + 1) * ny] = first
                outgoing[r, 1, p * ny : (p + 1) * ny] = second
            else:
                at = pl.ds(pl.multiple_of(d * rows + p * ny, ny), ny)
                incoming[0, at] = first
                incoming[1, at] = second
        if r + 1 < doms:
            send_terms(r + 1)

    for r in range(doms - 1, 0, -1):
        backs[r].wait_recv()
    result = pltpu.make_async_copy(incoming, moments_ref, out_sem)
    result.start()

    highs, lows = [], []
    for t in range(rows):
        values = jnp.concatenate(
            [incoming[m, pl.ds(t, doms, stride=rows), :] for m in range(2)], axis=0
        )
        high = values.astype(jnp.bfloat16)
        highs.append(high)
        lows.append((values - high.astype(jnp.float32)).astype(jnp.bfloat16))
    left = jnp.concatenate([jnp.concatenate(highs, axis=1), jnp.concatenate(lows, axis=1)], axis=0)
    dims = (((1,), (1,)), ((), ()))
    product = lax.dot_general(
        left, basis[0], dims, preferred_element_type=jnp.float32
    ) + lax.dot_general(left, basis[1], dims, preferred_element_type=jnp.float32)
    product = (product[: 2 * doms] + product[2 * doms :]) * (1.0 / (nx * ny * nz))
    partial[:, :vectors] = product
    gathered[d] = partial[...]

    copies = []
    for r in range(doms - 1, 0, -1):
        copy = pltpu.make_async_remote_copy(
            src_ref=partial,
            dst_ref=gathered.at[d],
            send_sem=dom_send.at[r],
            recv_sem=dom_recv.at[r],
            device_id={"dom": d ^ r},
            device_id_type=MESH,
        )
        copy.start()
        copies.append(copy)
    for copy in copies:
        copy.wait_recv()
    total = gathered[0]
    for e in range(1, doms):
        total = total + gathered[e]
    shared[g] = total
    spread = []
    for s in range(1, groups):
        copy = pltpu.make_async_remote_copy(
            src_ref=shared.at[g],
            dst_ref=shared.at[g],
            send_sem=node_send.at[s],
            recv_sem=node_recv.at[s],
            device_id={"node": lax.rem(g + s, groups)},
            device_id_type=MESH,
        )
        copy.start()
        spread.append(copy)
    for r in range(1, doms):
        for i in range(4):
            sends[r, i].wait_send()
        backs[r].wait_send()
    for copy in copies:
        copy.wait_send()
    for copy in spread:
        copy.wait()
    for n in range(groups):
        for m in range(2):
            projections_ref[m, n * doms : (n + 1) * doms, :] = shared[n, m * doms : (m + 1) * doms, :vectors]
    result.wait()


def fused(total, groups, doms, probes, slope, root, damping):
    vectors, planes, ny, nz = probes.shape
    rows, nx, half = planes * ny, planes * doms, total // 2
    anywhere = pl.BlockSpec(memory_space=pl.ANY)
    grid = (half, 2, nx + 2, ny + 16, nz)
    moments, projections = pl.pallas_call(
        functools.partial(kernel, contour(total), groups, doms, planes, ny),
        out_shape=(
            jax.ShapeDtypeStruct((2, doms * rows, nz), jnp.float32),
            jax.ShapeDtypeStruct((2, vectors, vectors), jnp.float32),
        ),
        in_specs=[anywhere] * 4,
        out_specs=(anywhere, pl.BlockSpec(memory_space=pltpu.VMEM)),
        scratch_shapes=[
            pltpu.VMEM((3, nx * ny, nz), jnp.float32),
            pltpu.VMEM((nx * ny, nz), jnp.float32),
            pltpu.VMEM((vectors * rows, nz), jnp.float32),
            pltpu.VMEM((2, vectors, rows * nz), jnp.bfloat16),
            pltpu.VMEM((half, 2, nx * ny, nz), jnp.float32),
            pltpu.VMEM(grid, jnp.float32),
            pltpu.VMEM(grid, jnp.float32),
            pltpu.VMEM((doms, 2, rows, nz), jnp.float32),
            pltpu.VMEM((2, doms * rows, nz), jnp.float32),
            pltpu.VMEM((2 * doms, 128), jnp.float32),
            pltpu.VMEM((doms, 2 * doms, 128), jnp.float32),
            pltpu.VMEM((groups, 2 * doms, 128), jnp.float32),
            pltpu.SemaphoreType.DMA((5,)),
            pltpu.SemaphoreType.DMA((doms, 4)),
            pltpu.SemaphoreType.DMA((doms, 4)),
            pltpu.SemaphoreType.DMA((doms,)),
            pltpu.SemaphoreType.DMA((doms,)),
            pltpu.SemaphoreType.DMA((doms,)),
            pltpu.SemaphoreType.DMA((doms,)),
            pltpu.SemaphoreType.DMA((groups,)),
            pltpu.SemaphoreType.DMA((groups,)),
            pltpu.SemaphoreType.DMA,
        ],
        compiler_params=pltpu.CompilerParams(collective_id=0, has_side_effects=True),
    )(
        probes.reshape(vectors * rows, nz),
        slope.reshape(rows, nz),
        root.reshape(rows, nz),
        damping.reshape(rows, nz),
    )
    moments = moments.reshape(2, 1, doms, planes, ny, nz)
    moments = jnp.pad(moments, ((0, 0), (0, 1)) + ((0, 0),) * 4)
    projections = jnp.pad(projections[:, None], ((0, 0), (0, 1), (0, 0), (0, 0)))
    return moments, projections


def solution(mesh):
    groups, doms = mesh.shape["node"], mesh.shape["dom"]

    def step(probes, slope, root, damping):
        vectors, ny = probes.shape[0], probes.shape[2]
        one_each = vectors == groups * doms and doms & (doms - 1) == 0 and doms % 8 == 0
        if one_each and ny % 8 == 0 and vectors <= 128 and probes.shape[3] % 128 == 0:
            return fused(NODE_DEV * groups, groups, doms, probes, slope, root, damping)
        return body(probes, slope, root, damping)

    in_specs = (
        P(None, "dom", None, None),
        P("dom", None, None),
        P("dom", None, None),
        P("dom", None, None),
    )
    out_specs = (P(None, None, "node", "dom", None, None), P())
    return jax.shard_map(step, mesh=mesh, in_specs=in_specs, out_specs=out_specs, check_vma=False)
```

```python
import functools
import math

import jax
import jax.numpy as jnp
from jax import lax
from jax.experimental import pallas as pl
from jax.experimental.pallas import tpu as pltpu
from jax.sharding import PartitionSpec as P

NODE_DEV = 2
SWEEPS = 8
UNROLL = 16


CENTRE = 0.5
RADIUS = 2.0


def grid_step(source, fields, factor_re, factor_im):
    padded = jnp.pad(fields, ((0, 0), (0, 0), (1, 1), (1, 1), (1, 1)))
    total = padded[:, :, 2:, 1:-1, 1:-1] + padded[:, :, :-2, 1:-1, 1:-1]
    total = total + padded[:, :, 1:-1, 2:, 1:-1] + padded[:, :, 1:-1, :-2, 1:-1]
    total = total + padded[:, :, 1:-1, 1:-1, 2:] + padded[:, :, 1:-1, 1:-1, :-2]
    real_part = source + total[:, 0]
    imag_part = total[:, 1]
    return jnp.stack(
        [
            real_part * factor_re - imag_part * factor_im,
            real_part * factor_im + imag_part * factor_re,
        ],
        axis=1,
    )


def inverse_diagonal(shift_real, shift_imaginary, slope, root, damping, guard):
    zr_col = shift_real[:, None, None, None, None]
    zi_col = shift_imaginary[:, None, None, None, None]
    decay = jnp.exp(-zr_col)
    real_d = slope * (zr_col - root) + damping * (decay * jnp.cos(zi_col))
    imag_d = slope * zi_col - damping * (decay * jnp.sin(zi_col))
    scale = 1.0 / (real_d * real_d + imag_d * imag_d + guard)
    return (real_d * scale, -imag_d * scale)


def per_system(fields, weight_re, weight_im):
    a_col = weight_re[:, None, None, None]
    b_col = weight_im[:, None, None, None]
    return jnp.stack(
        [a_col * fields[:, 0] - b_col * fields[:, 1], a_col * fields[:, 1] + b_col * fields[:, 0]]
    )


def body(probes, slope, root, damping):
    vectors = probes.shape[0]
    planes = probes.shape[1]
    groups = lax.axis_size("node")
    total = NODE_DEV * groups
    first = (lax.axis_index("node") * NODE_DEV).astype(jnp.float32)
    dom_size = lax.axis_size("dom")
    count = NODE_DEV * vectors // dom_size
    replicated = jnp.broadcast_to(probes[None], (NODE_DEV,) + probes.shape).reshape(
        (NODE_DEV * vectors,) + probes.shape[1:]
    )
    own = lax.all_to_all(replicated, "dom", split_axis=0, concat_axis=1, tiled=True)
    slope_all, root_all, damping_all = (
        lax.all_gather(slope, "dom", axis=0, tiled=True),
        lax.all_gather(root, "dom", axis=0, tiled=True),
        lax.all_gather(damping, "dom", axis=0, tiled=True),
    )
    system = lax.axis_index("dom") * count + jnp.arange(count)
    position = first + (system // vectors).astype(jnp.float32)
    theta = 2.0 * math.pi * (position + 0.5) / total
    shift_real = CENTRE + RADIUS * jnp.cos(theta)
    shift_imaginary = RADIUS * jnp.sin(theta)
    qre, qim = inverse_diagonal(
        shift_real, shift_imaginary, slope_all[None], root_all[None], damping_all[None], 0.0
    )
    qre = qre[:, 0]
    qim = qim[:, 0]
    fields = jnp.stack([own * qre, own * qim], axis=1)
    for sweep in range(SWEEPS):
        fields = grid_step(own, fields, qre, qim)
    weight_re = RADIUS * jnp.cos(theta) / total
    weight_im = RADIUS * jnp.sin(theta) / total
    shifted_re = weight_re * shift_real - weight_im * shift_imaginary
    shifted_im = weight_re * shift_imaginary + weight_im * shift_real
    terms = jnp.stack(
        [per_system(fields, weight_re, weight_im), per_system(fields, shifted_re, shifted_im)]
    )
    back = lax.all_to_all(terms, "dom", split_axis=3, concat_axis=2, tiled=True)
    local = jnp.sum(back.reshape((2, 2, NODE_DEV, vectors) + probes.shape[1:]), axis=2)
    flat = local.reshape(4 * vectors, -1)
    basis = probes.reshape(vectors, -1)
    partial_value = lax.dot_general(
        flat,
        basis,
        (((1,), (1,)), ((), ())),
        precision=lax.Precision.HIGHEST,
        preferred_element_type=jnp.float32,
    )
    cells = planes * probes.shape[2] * probes.shape[3] * lax.axis_size("dom")
    projections = lax.psum(partial_value.reshape(2, 2, vectors, vectors) / cells, ("node", "dom"))
    summed = lax.psum(local, "node")
    share = vectors // groups
    moments = lax.dynamic_slice_in_dim(summed, lax.axis_index("node") * share, share, 2)
    return (moments, projections)


MESH = pl.DeviceIdType.MESH


def contour(total):
    nodes = []
    for node in range(total // 2):
        theta = 2.0 * math.pi * (node + 0.5) / total
        zr, zi = CENTRE + RADIUS * math.cos(theta), RADIUS * math.sin(theta)
        wr, wi = RADIUS * math.cos(theta) / total, RADIUS * math.sin(theta) / total
        decay = math.exp(-zr)
        nodes.append(
            dict(
                zr=zr,
                zi=zi,
                er=decay * math.cos(zi),
                ei=decay * math.sin(zi),
                first=(2.0 * wr, 2.0 * wi),
                second=(2.0 * (wr * zr - wi * zi), 2.0 * (wr * zi + wi * zr)),
            )
        )
    return nodes


def kernel(
    nodes,
    groups,
    doms,
    planes,
    ny,
    probes_ref,
    slope_ref,
    root_ref,
    damping_ref,
    moments_ref,
    projections_ref,
    coef,
    rhs,
    local,
    basis,
    q,
    even,
    odd,
    outgoing,
    incoming,
    partial,
    gathered,
    own_sem,
    field_send,
    field_recv,
    term_send,
    term_recv,
    node_send,
    node_recv,
    out_sem,
):
    g = lax.axis_index("node")
    d = lax.axis_index("dom")
    rows = planes * ny
    half = len(nodes)
    nx = doms * planes
    nz = rhs.shape[-1]
    fields = (slope_ref, root_ref, damping_ref)

    barrier = pltpu.get_barrier_semaphore()
    for r in range(1, doms):
        pl.semaphore_signal(barrier, inc=1, device_id={"dom": d ^ r}, device_id_type=MESH)
    for s in range(1, groups):
        pl.semaphore_signal(
            barrier, inc=1, device_id={"node": lax.rem(g + s, groups)}, device_id_type=MESH
        )

    mine = pl.ds(pl.multiple_of(d * rows, rows), rows)
    own = [pltpu.make_async_copy(f, coef.at[i, mine], own_sem.at[i]) for i, f in enumerate(fields)]
    own.append(
        pltpu.make_async_copy(
            probes_ref.at[pl.ds((g * doms + d) * rows, rows)], rhs.at[mine], own_sem.at[3]
        )
    )
    whole_local = pltpu.make_async_copy(probes_ref, local, own_sem.at[4])
    for copy in own:
        copy.start()
    whole_local.start()
    pl.semaphore_wait(barrier, doms - 1 + groups - 1)

    sends = {}

    def send_field(r, i, src, dst):
        copy = pltpu.make_async_remote_copy(
            src_ref=src,
            dst_ref=dst,
            send_sem=field_send.at[r, i],
            recv_sem=field_recv.at[r, i],
            device_id={"dom": d ^ r},
            device_id_type=MESH,
        )
        copy.start()
        sends[r, i] = copy

    for r in list(range(doms - 2, 0, -2)) + [1]:
        for i, f in enumerate(fields):
            send_field(r, i, f, coef.at[i, mine])
    for r in range(doms - 1, 0, -1):
        source = probes_ref.at[pl.ds((g * doms + (d ^ r)) * rows, rows)]
        send_field(r, 3, source, rhs.at[mine])

    blank = jnp.zeros((2, 8, nz), jnp.float32)
    for buffer in (even, odd):
        for k in range(half):
            for end in (0, nx + 1):
                buffer[k, :, end] = jnp.zeros((2, ny + 16, nz), jnp.float32)

            def clear(x, _, buffer=buffer, k=k):
                buffer[k, :, x, 0:8] = blank
                buffer[k, :, x, ny + 8 : ny + 16] = blank
                return 0

            lax.fori_loop(1, nx + 1, clear, 0)

    lane = lax.broadcasted_iota(jnp.int32, (ny, nz), 1)
    first_lane, last_lane = lane == 0, lane == nz - 1

    def start_plane(x):
        at = pl.ds(pl.multiple_of(x * ny, ny), ny)
        slope, root, damping = coef[0, at], coef[1, at], coef[2, at]
        b = rhs[at]
        for k, c in enumerate(nodes):
            re = slope * (c["zr"] - root) + damping * c["er"]
            im = slope * c["zi"] - damping * c["ei"]
            scale = 1.0 / (re * re + im * im)
            re = re * scale
            im = -im * scale
            q[k, 0, at] = re
            q[k, 1, at] = im
            even[k, 0, x + 1, 8 : ny + 8] = b * re
            even[k, 1, x + 1, 8 : ny + 8] = b * im

    for copy in own:
        copy.wait()
    for p in range(planes):
        start_plane(d * planes + p)

    whole_local.wait()
    vectors = local.shape[0] // rows
    for t in range(rows):
        values = local[pl.ds(t, vectors, stride=rows), :]
        high = values.astype(jnp.bfloat16)
        low = (values - high.astype(jnp.float32)).astype(jnp.bfloat16)
        basis[0, :, t * nz : (t + 1) * nz] = high
        basis[1, :, t * nz : (t + 1) * nz] = low

    relays = {}
    for r in range(2, doms, 2):
        at = pl.ds(pl.multiple_of((d ^ r) * rows, rows), rows)
        for i in range(3):
            sends[r, i].wait_recv()
            copy = pltpu.make_async_remote_copy(
                src_ref=coef.at[i, at],
                dst_ref=coef.at[i, at],
                send_sem=field_send.at[r + 1, i],
                recv_sem=field_recv.at[r + 1, i],
                device_id={"dom": d ^ 1},
                device_id_type=MESH,
            )
            copy.start()
            relays[r + 1, i] = copy
    for r in [1] + list(range(2, doms, 2)) + list(range(3, doms, 2)):
        if r == 1:
            for i in range(3):
                sends[r, i].wait_recv()
        elif r % 2:
            for i in range(3):
                relays[r, i].wait_recv()
        sends[r, 3].wait_recv()
        for p in range(planes):
            start_plane((d ^ r) * planes + p)

    def neighbours(source, k, c, x):
        centre = source[k, c, x + 1, 8 : ny + 8]
        total = source[k, c, x, 8 : ny + 8] + source[k, c, x + 2, 8 : ny + 8]
        total = total + (source[k, c, x + 1, 7 : ny + 7] + source[k, c, x + 1, 9 : ny + 9])
        before = jnp.where(first_lane, 0.0, pltpu.roll(centre, 1, 1))
        after = jnp.where(last_lane, 0.0, pltpu.roll(centre, nz - 1, 1))
        return total + (before + after)

    def update(source, k, x, b):
        at = pl.ds(pl.multiple_of(x * ny, ny), ny)
        re = b + neighbours(source, k, 0, x)
        im = neighbours(source, k, 1, x)
        qre, qim = q[k, 0, at], q[k, 1, at]
        return re * qre - im * qim, re * qim + im * qre

    def sweep(source, target):
        unroll = math.gcd(UNROLL, nx)

        def step(i, _):
            for u in range(unroll):
                x = i * unroll + u
                b = rhs[pl.ds(pl.multiple_of(x * ny, ny), ny)]
                for k in range(half):
                    re, im = update(source, k, x, b)
                    target[k, 0, x + 1, 8 : ny + 8] = re
                    target[k, 1, x + 1, 8 : ny + 8] = im
            return 0

        lax.fori_loop(0, nx // unroll, step, 0)

    def pair(_, carry):
        sweep(even, odd)
        sweep(odd, even)
        return carry

    lax.fori_loop(0, (SWEEPS - 1) // 2, pair, 0)
    source = even
    if (SWEEPS - 1) % 2:
        sweep(even, odd)
        source = odd

    backs = {}

    def send_terms(r):
        copy = pltpu.make_async_remote_copy(
            src_ref=outgoing.at[r],
            dst_ref=incoming.at[:, mine],
            send_sem=term_send.at[r],
            recv_sem=term_recv.at[r],
            device_id={"dom": d ^ r},
            device_id_type=MESH,
        )
        copy.start()
        backs[r] = copy

    for r in range(doms - 1, -1, -1):
        for p in range(planes):
            x = (d ^ r) * planes + p
            b = rhs[pl.ds(pl.multiple_of(x * ny, ny), ny)]
            first = second = None
            for k, c in enumerate(nodes):
                re, im = update(source, k, x, b)
                one = re * c["first"][0] - im * c["first"][1]
                two = re * c["second"][0] - im * c["second"][1]
                first = one if first is None else first + one
                second = two if second is None else second + two
            if r:
                outgoing[r, 0, p * ny : (p + 1) * ny] = first
                outgoing[r, 1, p * ny : (p + 1) * ny] = second
            else:
                at = pl.ds(pl.multiple_of(d * rows + p * ny, ny), ny)
                incoming[0, at] = first
                incoming[1, at] = second
        if r + 1 < doms:
            send_terms(r + 1)

    for r in range(doms - 1, 0, -1):
        backs[r].wait_recv()
    result = pltpu.make_async_copy(incoming, moments_ref, out_sem)
    result.start()

    highs, lows = [], []
    for t in range(rows):
        values = jnp.concatenate(
            [incoming[m, pl.ds(t, doms, stride=rows), :] for m in range(2)], axis=0
        )
        high = values.astype(jnp.bfloat16)
        highs.append(high)
        lows.append((values - high.astype(jnp.float32)).astype(jnp.bfloat16))
    left = jnp.concatenate([jnp.concatenate(highs, axis=1), jnp.concatenate(lows, axis=1)], axis=0)
    dims = (((1,), (1,)), ((), ()))
    product = lax.dot_general(
        left, basis[0], dims, preferred_element_type=jnp.float32
    ) + lax.dot_general(left, basis[1], dims, preferred_element_type=jnp.float32)
    product = (product[: 2 * doms] + product[2 * doms :]) * (1.0 / (nx * ny * nz))
    packs = partial.shape[1] // vectors
    height = 2 * doms // packs
    for n in range(packs):
        partial[:, n * vectors : (n + 1) * vectors] = product[n * height : (n + 1) * height]
    gathered[g, d] = partial[...]

    copies = []
    for s in [*range(groups // 2, 0, -1), *range(groups // 2 + 1, groups), 0]:
        for r in range(doms - 1, -1, -1):
            if s or r:
                copy = pltpu.make_async_remote_copy(
                    src_ref=partial,
                    dst_ref=gathered.at[g, d],
                    send_sem=node_send.at[s, r],
                    recv_sem=node_recv.at[s, r],
                    device_id={"node": lax.rem(g + s, groups), "dom": d ^ r},
                    device_id_type=MESH,
                )
                copy.start()
                copies.append(copy)
    for r in range(1, doms):
        backs[r].wait_send()
    for copy in list(sends.values()) + list(relays.values()):
        copy.wait_send()
    for copy in copies:
        copy.wait()
    for n in range(groups):
        total = gathered[n, 0]
        for e in range(1, doms):
            total = total + gathered[n, e]
        for k in range(packs):
            m, j = divmod(k * height, doms)
            projections_ref[m, n * doms + j : n * doms + j + height, :] = total[:, k * vectors : (k + 1) * vectors]
    result.wait()


def fused(total, groups, doms, probes, slope, root, damping):
    vectors, planes, ny, nz = probes.shape
    rows, nx, half = planes * ny, planes * doms, total // 2
    anywhere = pl.BlockSpec(memory_space=pl.ANY)
    grid = (half, 2, nx + 2, ny + 16, nz)
    moments, projections = pl.pallas_call(
        functools.partial(kernel, contour(total), groups, doms, planes, ny),
        out_shape=(
            jax.ShapeDtypeStruct((2, doms * rows, nz), jnp.float32),
            jax.ShapeDtypeStruct((2, vectors, vectors), jnp.float32),
        ),
        in_specs=[anywhere] * 4,
        out_specs=(anywhere, pl.BlockSpec(memory_space=pltpu.VMEM)),
        scratch_shapes=[
            pltpu.VMEM((3, nx * ny, nz), jnp.float32),
            pltpu.VMEM((nx * ny, nz), jnp.float32),
            pltpu.VMEM((vectors * rows, nz), jnp.float32),
            pltpu.VMEM((2, vectors, rows * nz), jnp.bfloat16),
            pltpu.VMEM((half, 2, nx * ny, nz), jnp.float32),
            pltpu.VMEM(grid, jnp.float32),
            pltpu.VMEM(grid, jnp.float32),
            pltpu.VMEM((doms, 2, rows, nz), jnp.float32),
            pltpu.VMEM((2, doms * rows, nz), jnp.float32),
            pltpu.VMEM((2 * doms * vectors // 128, 128), jnp.float32),
            pltpu.VMEM((groups, doms, 2 * doms * vectors // 128, 128), jnp.float32),
            pltpu.SemaphoreType.DMA((5,)),
            pltpu.SemaphoreType.DMA((doms, 4)),
            pltpu.SemaphoreType.DMA((doms, 4)),
            pltpu.SemaphoreType.DMA((doms,)),
            pltpu.SemaphoreType.DMA((doms,)),
            pltpu.SemaphoreType.DMA((groups, doms)),
            pltpu.SemaphoreType.DMA((groups, doms)),
            pltpu.SemaphoreType.DMA,
        ],
        compiler_params=pltpu.CompilerParams(collective_id=0, has_side_effects=True),
    )(
        probes.reshape(vectors * rows, nz),
        slope.reshape(rows, nz),
        root.reshape(rows, nz),
        damping.reshape(rows, nz),
    )
    moments = moments.reshape(2, 1, doms, planes, ny, nz)
    moments = jnp.pad(moments, ((0, 0), (0, 1)) + ((0, 0),) * 4)
    projections = jnp.pad(projections[:, None], ((0, 0), (0, 1), (0, 0), (0, 0)))
    return moments, projections


def solution(mesh):
    groups, doms = mesh.shape["node"], mesh.shape["dom"]

    def step(probes, slope, root, damping):
        vectors, ny = probes.shape[0], probes.shape[2]
        one_each = vectors == groups * doms and doms & (doms - 1) == 0 and doms % 8 == 0
        if one_each and ny % 8 == 0 and 128 % vectors == 0 and probes.shape[3] % 128 == 0:
            return fused(NODE_DEV * groups, groups, doms, probes, slope, root, damping)
        return body(probes, slope, root, damping)

    in_specs = (
        P(None, "dom", None, None),
        P("dom", None, None),
        P("dom", None, None),
        P("dom", None, None),
    )
    out_specs = (P(None, None, "node", "dom", None, None), P())
    return jax.shard_map(step, mesh=mesh, in_specs=in_specs, out_specs=out_specs, check_vma=False)
```
